32 devices in a mesh: blk: 8 (over y, x, core), team: 4 (over z).
Axes of the slice: x: 2, y: 2, z: 4, core: 2. Of those that a mesh axis runs over, the one named last changes fastest.
Arguments:
- features: bfloat16 [8192, 128], P(('blk', 'team')), may hold values from -0.796875 to 0.796875
- left_vectors: bfloat16 [8192, 128], P(('blk', 'team')), may hold values from -0.8984375 to 0.8984375
- right_vectors: bfloat16 [8192, 128], P(('blk', 'team')), may hold values from -0.8984375 to 0.8984375
Outputs:
- feature_grad: float32 [8192, 128], P(('blk', 'team'))
The draws below stay inside these ranges and needn't reach their ends.
All inputs are finite; a program needn't handle non-finite values.
Results may differ from the reference program's by a relative error of at most 0.0039.
Values may be sent and summed in bfloat16 or wider, within the bound.
A program may use at most 64 MiB of HBM per device.

```python
import jax
import jax.numpy as jnp
from jax import lax

FEAT = 128
VEC = 128
POINTS = 8192


def steps_of(own_key, dims, pieces, least, high):
    gain, own = 1.0, jax.random.fold_in(own_key, 6)
    for position, parts in pieces:
        draws = jnp.exp(jax.random.uniform(jax.random.fold_in(own, position), (parts,), jnp.float32, least / len(pieces), high / len(pieces)))
        gain = gain * jnp.repeat(draws, dims[position] // parts).reshape([-1 if axis == position else 1 for axis in range(len(dims))])
    return gain


def normal_values(rng, dims, scale, reach, shards=(), kind=jnp.bfloat16):
    factor_of = steps_of(rng, dims, shards, -0.22, 0.18) if shards else 1.0
    drawn = jax.random.normal(rng, dims, jnp.float32) * scale * factor_of
    return jnp.minimum(jnp.maximum(drawn, -reach), reach).astype(kind)


def setup_inputs(seed: int = 0) -> dict:
    splits = jax.random.split(jax.random.key(seed), 4)
    return {
        "features": normal_values(splits[0], (POINTS, FEAT), 0.1, 0.796875, ((0, 32),)),
        "left_vectors": normal_values(splits[1], (POINTS, VEC), 0.11, 0.8984375, ((0, 32),)),
        "right_vectors": normal_values(splits[2], (POINTS, VEC), 0.11, 0.8984375, ((0, 32),)),
    }


def pair_block(target_x, target_l, target_r, target_norm, source_x, source_l, source_r, source_norm):
    cross = jnp.dot(target_x, source_x.T, preferred_element_type=jnp.float32)
    dist_sq = target_norm[:, None] + source_norm[None, :] - 2.0 * cross
    radius = jnp.sqrt(jnp.maximum(dist_sq, 0.0))
    couple = jnp.dot(target_l, source_r.T, preferred_element_type=jnp.float32) + jnp.dot(target_r, source_l.T, preferred_element_type=jnp.float32)
    root_five = jnp.float32(5.0) ** 0.5
    weight = (-(5.0 / 3.0) * (1.0 + root_five * radius) * jnp.exp(-root_five * radius) * couple).astype(jnp.bfloat16)
    row_total = lax.optimization_barrier(jnp.sum(weight.astype(jnp.float32), axis=1))
    return row_total[:, None] * target_x.astype(jnp.float32) - jnp.dot(weight, source_x, preferred_element_type=jnp.float32)

def reference(features, left_vectors, right_vectors):
    total = features.shape[0]
    width = min(512, total)
    norms = lax.optimization_barrier(jnp.sum(features.astype(jnp.float32) ** 2, axis=1))
    count_blocks = total // width

    def one_block(packed):
        block_x, block_l, block_r, block_norm = packed
        return pair_block(block_x, block_l, block_r, block_norm, features, left_vectors, right_vectors, norms)
    result = lax.map(one_block, (features.reshape(count_blocks, width, -1), left_vectors.reshape(count_blocks, width, -1), right_vectors.reshape(count_blocks, width, -1), norms.reshape(count_blocks, width)))
    return result.reshape(total, -1)
```

```python
import functools
import math

import jax
import jax.numpy as jnp
from jax import lax
from jax.experimental import pallas as pl
from jax.experimental.pallas import tpu as pltpu
from jax.sharding import PartitionSpec as P

MESH = pl.DeviceIdType.MESH
LOG2E = math.log2(math.e)
RATE = math.sqrt(5.0) * LOG2E
GAIN = -(5.0 / 3.0) / LOG2E
NT = (((1,), (1,)), ((), ()))
ONES = 16


def flip(index, bits):
    step = 1
    while step <= bits:
        if bits & step:
            index = index + step - 2 * step * ((index // step) % 2)
        step *= 2
    return index


def columns(norm, lane, first, ones):
    high = norm.astype(jnp.bfloat16).astype(jnp.float32)
    rest = norm - high
    mid = rest.astype(jnp.bfloat16).astype(jnp.float32)
    low = rest - mid
    out = jnp.where((lane >= ones) & (lane < ones + 3), 1.0, 0.0)
    for place, term in enumerate((high, mid, low)):
        out = jnp.where(lane == first + place, term, out)
    return out.astype(jnp.bfloat16)


def goes_up(teams, i):
    return 2 * i <= teams - 2


def goes_down(teams, i):
    return 2 * i > teams


def above(teams, i, t):
    return (t > i) & (t <= teams - 1 - i)


def below(teams, i, t):
    return (t < i) & (t > teams - 1 - i)


def kernel(
    planes, teams, parts, x_hbm, l_hbm, r_hbm, out_ref,
    own, tgt, src, tgt_left, tgt_turned, src_right, acc, turned,
    core_out, core_in, plane_out, plane_in, line_out, line_in, mine_out,
    out_sem, load_sem, core_send, core_recv, plane_send, plane_recv,
    own_send, line_send, line_recv, csum_send, csum_recv,
    psum_send, psum_recv, lsum_send, lsum_recv,
):
    blk, team = lax.axis_index("blk"), lax.axis_index("team")
    plane, core = blk // 2, blk % 2
    rows, feat = x_hbm.shape
    half, size = rows // 2, rows // parts
    bf16, f32 = jnp.bfloat16, jnp.float32

    loads = [
        pltpu.make_async_copy(ref, own.at[i], load_sem.at[i])
        for i, ref in enumerate((x_hbm, l_hbm, r_hbm))
    ]
    for load in loads:
        load.start()

    partner = (plane * 2 + 1 - core, team)
    peer = [(flip(plane, k) * 2 + core, team) for k in range(planes)]
    single = [k for k in range(1, planes) if k & (k - 1) == 0]
    joint = [k for k in range(1, planes) if k & (k - 1)]
    barrier = pltpu.get_barrier_semaphore()
    near = [partner] + [peer[k] for k in single]
    for device in near:
        pl.semaphore_signal(barrier, inc=1, device_id=device, device_id_type=MESH)
    for step in (1, -1):
        @pl.when((team + step >= 0) & (team + step < teams))
        def _():
            pl.semaphore_signal(barrier, inc=1, device_id=(blk, team + step), device_id_type=MESH)

    def remote(source, target, send, recv, device):
        return pltpu.make_async_remote_copy(
            src_ref=source, dst_ref=target, send_sem=send, recv_sem=recv,
            device_id=device, device_id_type=MESH,
        )

    def raw(k, c):
        return own if (k, c) == (0, 0) else tgt.at[k, c]

    def part(ref, h, length):
        return ref.at[:, pl.ds(h * length, length)]

    def plane_copy(k, h):
        if k in single:
            source, device = own, peer[k]
        else:
            low = k & -k
            rest = k ^ low
            if h and rest in single:
                source, device = raw(low, 0), peer[rest]
            else:
                source, device = raw(rest, 0), peer[low]
        return remote(
            part(source, h, half), part(tgt.at[k, 0], h, half),
            plane_send.at[k, h], plane_recv.at[k, h], device,
        )

    def core_copy(k):
        return remote(raw(k, 0), tgt.at[k, 1], core_send.at[k], core_recv.at[k], partner)

    sources = [i for i in range(teams) if goes_up(teams, i) or goes_down(teams, i)]
    sources.sort(key=lambda i: (min(i, teams - 1 - i), i))

    def direction(i):
        return 1 if goes_up(teams, i) else -1

    def uses(i, t):
        return above(teams, i, t) if goes_up(teams, i) else below(teams, i, t)

    def passes(i):
        return uses(i, team) & uses(i, team + direction(i))

    def line_copy(i, q):
        return remote(
            part(src.at[i], q, size), part(src.at[i], q, size),
            line_send.at[i, q], line_recv.at[i, q], (blk, team + direction(i)),
        )

    def own_copy(step, q):
        return remote(
            part(own, q, size), part(src.at[team], q, size),
            own_send.at[q], line_recv.at[team, q], (blk, team + step),
        )

    rises = goes_up(teams, team)
    sinks = goes_down(teams, team)

    def send_own(qs):
        for step, condition in ((1, rises), (-1, sinks)):
            @pl.when(condition)
            def _():
                for q in qs:
                    own_copy(step, q).start()

    def pass_on(q):
        for i in sources:
            @pl.when(passes(i))
            def _():
                line_copy(i, q).wait_recv()
                line_copy(i, q).start()

    for load in loads:
        load.wait()
    on_line = jnp.minimum(team, 1) + jnp.minimum(teams - 1 - team, 1)
    pl.semaphore_wait(barrier, len(near) + on_line)
    edge = (team == 0) | (team == teams - 1)
    send_own(range(1))

    @pl.when(edge)
    def _():
        send_own(range(1, parts))
    for n, k in enumerate(single):
        plane_copy(k, 1 - n % 2).start()
    core_copy(0).start()
    for n, k in enumerate(single):
        plane_copy(k, n % 2).start()

    lane = lax.broadcasted_iota(jnp.int32, (rows, feat), 1)
    one_row = jnp.where(lax.broadcasted_iota(jnp.int32, (ONES, rows), 0) == 0, 1.0, 0.0).astype(bf16)

    def norm_of(x):
        xf = x.astype(f32)
        return jnp.sum(xf * xf, axis=1, keepdims=True)

    def prepare_target(k, c):
        x = raw(k, c)[0]
        tgt_left[k, c, :, :feat] = x * bf16(-2.0)
        tgt_left[k, c, :, feat:] = columns(norm_of(x), lane, 0, 3)
        tgt_turned[k, c, :feat] = x.astype(f32).T.astype(bf16)
        tgt_turned[k, c, feat:] = one_row

    def prepare_source(ref, slot):
        x = ref[0]
        src_right[slot, :, :feat] = x
        src_right[slot, :, feat:] = columns(norm_of(x), lane, 3, 0)

    mine = teams

    def pair(k, c, ref, slot, add, first):
        right = src_right[slot]
        target = raw(k, c)
        dist = lax.dot_general(tgt_left[k, c], right, NT, preferred_element_type=f32)
        couple = lax.dot_general(
            jnp.concatenate([target[1], target[2]], axis=1),
            jnp.concatenate([ref[2], ref[1]], axis=1),
            NT, preferred_element_type=f32,
        )
        dist = jnp.maximum(dist, 1e-30)
        power = dist * lax.rsqrt(dist) * (-RATE)
        weight = ((LOG2E - power) * jnp.exp2(power) * couple).astype(bf16)
        back = jnp.dot(tgt_turned[k, c], weight, preferred_element_type=f32)
        if first:
            turned[slot] = back
        else:
            turned[slot] += back
        if add is not None:
            forth = jnp.dot(weight, right, preferred_element_type=f32)
            if add:
                acc[k, c] += forth
            else:
                acc[k, c] = forth

    def gradient(k, c):
        total = acc[k, c]
        return GAIN * (total[:, feat:feat + 1] * raw(k, c)[0].astype(f32) - total[:, :feat])

    def turned_gradient(ref, slot):
        total = turned[slot]
        fill = jnp.zeros((feat - ONES, rows), f32)
        whole = jnp.concatenate([total, fill], axis=0).T
        return GAIN * (whole[:, feat:feat + 1] * ref[0].astype(f32) - whole[:, :feat])

    def with_own(k, c):
        prepare_target(k, c)
        pair(k, c, own, mine, None, (k, c) == (0, 0))

    prepare_source(own, mine)
    with_own(0, 0)
    pass_on(0)
    core_copy(0).wait_recv()
    with_own(0, 1)

    started = set()
    arrived = set()

    def arrive(k, h):
        if (k, h) not in arrived:
            arrived.add((k, h))
            plane_copy(k, h).wait_recv()

    def hand_on(k):
        low = k & -k
        rest = k ^ low
        arrive(rest, 0)
        plane_copy(k, 0).start()
        arrive(low if rest in single else rest, 1)
        plane_copy(k, 1).start()

    middle = [q for q in range(1, parts)]
    for k in joint:
        if bin(k).count("1") == 2:
            hand_on(k)
    for q in middle[:-1]:
        pass_on(q)
    for k in single:
        arrive(k, 0)
        arrive(k, 1)
        core_copy(k).start()
    for k in single:
        with_own(k, 0)
    for q in middle[-1:]:
        pass_on(q)

    @pl.when(jnp.logical_not(edge))
    def _():
        send_own(range(1, parts))
    for k in single:
        core_copy(k).wait_recv()
        with_own(k, 1)
    for k in joint:
        if bin(k).count("1") > 2:
            hand_on(k)
        arrive(k, 0)
        arrive(k, 1)
        core_copy(k).start()
        with_own(k, 0)
    for k in joint:
        core_copy(k).wait_recv()
        with_own(k, 1)

    def to_owner(i):
        return remote(
            line_out.at[i], line_in.at[team], lsum_send.at[i], lsum_recv.at[team], (blk, i),
        )

    for n, i in enumerate(sources):
        @pl.when(uses(i, team))
        def _():
            @pl.when(jnp.logical_not(passes(i)))
            def _():
                for q in range(parts):
                    line_copy(i, q).wait_recv()
            prepare_source(src.at[i], i)
            for k in reversed(range(planes)):
                for c in (1, 0):
                    pair(k, c, src.at[i], i, n > 0, (k, c) == (planes - 1, 1))
            line_out[i] = turned_gradient(src.at[i], i).astype(bf16)
            to_owner(i).start()

    def csum_copy(k):
        return remote(core_out.at[k], core_in.at[k], csum_send.at[k], csum_recv.at[k], partner)

    def psum_copy(k):
        return remote(plane_out.at[k - 1], plane_in.at[k - 1], psum_send.at[k], psum_recv.at[k], peer[k])

    mine_out[...] = turned_gradient(own, mine)

    @pl.when(team > 0)
    def _():
        for k in reversed(range(planes)):
            core_out[k] = gradient(k, 1).astype(bf16)
            csum_copy(k).start()
        for k in reversed(range(1, planes)):
            csum_copy(k).wait_recv()
            plane_out[k - 1] = (gradient(k, 0) + core_in[k].astype(f32)).astype(bf16)
            psum_copy(k).start()
        csum_copy(0).wait_recv()
        mine_out[...] += gradient(0, 0) + core_in[0].astype(f32)
        for k in range(1, planes):
            psum_copy(k).wait_recv()
            mine_out[...] += plane_in[k - 1].astype(f32)

    def gives(j):
        return (rises & above(teams, team, j)) | (sinks & below(teams, team, j))

    for j in range(teams):
        @pl.when(gives(j))
        def _():
            remote(line_out.at[j], line_in.at[j], lsum_send.at[j], lsum_recv.at[j], partner).wait_recv()
            mine_out[...] += line_in[j].astype(f32)
    put = pltpu.make_async_copy(mine_out, out_ref, out_sem)
    put.start()
    put.wait()

    for k in range(1, planes):
        for h in range(2):
            plane_copy(k, h).wait_send()
    for k in range(planes):
        core_copy(k).wait_send()
    for step, condition in ((1, rises), (-1, sinks)):
        @pl.when(condition)
        def _():
            for q in range(parts):
                own_copy(step, q).wait_send()
    for i in sources:
        @pl.when(passes(i))
        def _():
            for q in range(parts):
                line_copy(i, q).wait_send()

        @pl.when(uses(i, team))
        def _():
            to_owner(i).wait_send()

    @pl.when(team > 0)
    def _():
        for k in range(planes):
            csum_copy(k).wait_send()
            if k:
                psum_copy(k).wait_send()


def local(planes, teams, features, left_vectors, right_vectors):
    rows, feat = features.shape
    kind = jnp.bfloat16
    dma = pltpu.SemaphoreType.DMA
    parts = 4
    others = max(planes - 1, 1)
    return pl.pallas_call(
        functools.partial(kernel, planes, teams, parts),
        out_shape=jax.ShapeDtypeStruct((rows, feat), jnp.float32),
        in_specs=[pl.BlockSpec(memory_space=pl.ANY)] * 3,
        out_specs=pl.BlockSpec(memory_space=pl.ANY),
        scratch_shapes=[
            pltpu.VMEM((3, rows, feat), kind),
            pltpu.VMEM((planes, 2, 3, rows, feat), kind),
            pltpu.VMEM((teams, 3, rows, feat), kind),
            pltpu.VMEM((planes, 2, rows, 2 * feat), kind),
            pltpu.VMEM((planes, 2, feat + ONES, rows), kind),
            pltpu.VMEM((teams + 1, rows, 2 * feat), kind),
            pltpu.VMEM((planes, 2, rows, 2 * feat), jnp.float32),
            pltpu.VMEM((teams + 1, feat + ONES, rows), jnp.float32),
            pltpu.VMEM((planes, rows, feat), kind),
            pltpu.VMEM((planes, rows, feat), kind),
            pltpu.VMEM((others, rows, feat), kind),
            pltpu.VMEM((others, rows, feat), kind),
            pltpu.VMEM((teams, rows, feat), kind),
            pltpu.VMEM((teams, rows, feat), kind),
            pltpu.VMEM((rows, feat), jnp.float32),
            dma,
            dma((3,)),
            dma((planes,)), dma((planes,)),
            dma((planes, 2)), dma((planes, 2)),
            dma((parts,)),
            dma((teams, parts)), dma((teams, parts)),
            dma((planes,)), dma((planes,)),
            dma((planes,)), dma((planes,)),
            dma((teams,)), dma((teams,)),
        ],
        compiler_params=pltpu.CompilerParams(collective_id=0, has_side_effects=True),
    )(features, left_vectors, right_vectors)


def solution(mesh):
    spec = P(("blk", "team"), None)
    planes, teams = mesh.shape["blk"] // 2, mesh.shape["team"]
    return jax.shard_map(
        functools.partial(local, planes, teams), mesh=mesh,
        in_specs=(spec, spec, spec), out_specs=spec, check_vma=False,
    )
```

```python
import functools
import math

import jax
import jax.numpy as jnp
from jax import lax
from jax.experimental import pallas as pl
from jax.experimental.pallas import tpu as pltpu
from jax.sharding import PartitionSpec as P

MESH = pl.DeviceIdType.MESH
LOG2E = math.log2(math.e)
RATE = math.sqrt(5.0) * LOG2E
GAIN = -(5.0 / 3.0) / LOG2E
NT = (((1,), (1,)), ((), ()))
ONES = 16


def flip(index, bits):
    step = 1
    while step <= bits:
        if bits & step:
            index = index + step - 2 * step * ((index // step) % 2)
        step *= 2
    return index


def columns(norm, lane, first, ones):
    high = norm.astype(jnp.bfloat16).astype(jnp.float32)
    rest = norm - high
    mid = rest.astype(jnp.bfloat16).astype(jnp.float32)
    low = rest - mid
    out = jnp.where((lane >= ones) & (lane < ones + 3), 1.0, 0.0)
    for place, term in enumerate((high, mid, low)):
        out = jnp.where(lane == first + place, term, out)
    return out.astype(jnp.bfloat16)


def top(teams, i):
    return teams - 1 - i - jnp.minimum(i, 1)


def bottom(teams, i):
    return jnp.maximum(teams - 1 - i, 1)


def rises(teams, i):
    return i + 1 <= top(teams, i)


def sinks(teams, i):
    return i - 1 >= bottom(teams, i)


def uses(teams, i, t):
    return ((t > i) & (t <= top(teams, i))) | ((t < i) & (t >= bottom(teams, i)))


def kernel(
    planes, teams, parts, x_hbm, l_hbm, r_hbm, out_ref,
    own, tgt, src, tgt_left, tgt_turned, src_right, acc, turned,
    core_out, core_in, plane_out, plane_in, line_out, line_in,
    load_sem, core_send, core_recv, plane_send, plane_recv,
    own_send, line_send, line_recv, csum_send, csum_recv,
    psum_send, psum_recv, lsum_send, lsum_recv,
):
    blk, team = lax.axis_index("blk"), lax.axis_index("team")
    plane, core = blk // 2, blk % 2
    rows, feat = x_hbm.shape
    half, size = rows // 2, rows // parts
    bf16, f32 = jnp.bfloat16, jnp.float32

    loads = [
        pltpu.make_async_copy(ref, own.at[i], load_sem.at[i])
        for i, ref in enumerate((x_hbm, l_hbm, r_hbm))
    ]
    for load in loads:
        load.start()

    partner = (plane * 2 + 1 - core, team)
    peer = [(flip(plane, k) * 2 + core, team) for k in range(planes)]
    single = [k for k in range(1, planes) if k & (k - 1) == 0]
    joint = [k for k in range(1, planes) if k & (k - 1)]
    barrier = pltpu.get_barrier_semaphore()
    near = [partner] + [peer[k] for k in single]
    for device in near:
        pl.semaphore_signal(barrier, inc=1, device_id=device, device_id_type=MESH)
    for step in (1, -1):
        @pl.when((team + step >= 0) & (team + step < teams))
        def _():
            pl.semaphore_signal(barrier, inc=1, device_id=(blk, team + step), device_id_type=MESH)

    def remote(source, target, send, recv, device):
        return pltpu.make_async_remote_copy(
            src_ref=source, dst_ref=target, send_sem=send, recv_sem=recv,
            device_id=device, device_id_type=MESH,
        )

    def raw(k, c):
        return own if (k, c) == (0, 0) else tgt.at[k, c]

    def part(ref, h, length):
        return ref.at[:, pl.ds(h * length, length)]

    inputs = (x_hbm, l_hbm, r_hbm)

    def straight(target, h, length, send, recv, device):
        for i, ref in enumerate(inputs):
            place = pl.ds(h * length, length)
            remote(ref.at[place], target.at[i, place], send, recv, device).start()

    def plane_copy(k, h):
        if k in single:
            source, device = own, peer[k]
        else:
            low = k & -k
            rest = k ^ low
            if h and rest in single:
                source, device = raw(low, 0), peer[rest]
            else:
                source, device = raw(rest, 0), peer[low]
        return remote(
            part(source, h, half), part(tgt.at[k, 0], h, half),
            plane_send.at[k, h], plane_recv.at[k, h], device,
        )

    def core_copy(k):
        return remote(raw(k, 0), tgt.at[k, 1], core_send.at[k], core_recv.at[k], partner)

    def direction(i):
        return 1 if 2 * i < teams - 1 else -1

    def goes(i):
        near_end, far_end = min(i, teams - 1 - i), max(i, teams - 1 - i)
        if i < far_end:
            return far_end - near_end > 1 or i == 0
        return far_end - near_end > 1 or 0 < near_end < far_end

    sources = [i for i in range(teams) if teams > 1 and goes(i)]

    def used(i):
        return uses(teams, i, team)

    def passes(i):
        return used(i) & uses(teams, i, team + direction(i))

    def line_copy(i, q):
        return remote(
            part(src.at[i], q, size), part(src.at[i], q, size),
            line_send.at[i, q], line_recv.at[i, q], (blk, team + direction(i)),
        )

    def own_copy(step, q):
        return remote(
            part(own, q, size), part(src.at[team], q, size),
            own_send.at[q], line_recv.at[team, q], (blk, team + step),
        )

    ways = ((1, rises(teams, team)), (-1, sinks(teams, team)))

    def pass_on(q, condition):
        for i in sources:
            @pl.when(passes(i) & condition)
            def _():
                line_copy(i, q).wait_recv()
                line_copy(i, q).start()

    on_line = jnp.minimum(team, 1) + jnp.minimum(teams - 1 - team, 1)
    pl.semaphore_wait(barrier, len(near) + on_line)
    for step, condition in ways:
        @pl.when(condition)
        def _():
            for q in range(parts):
                straight(
                    src.at[team], q, size, own_send.at[q], line_recv.at[team, q], (blk, team + step),
                )

    def to_plane(k, h):
        straight(tgt.at[k, 0], h, half, plane_send.at[k, h], plane_recv.at[k, h], peer[k])

    for n, k in enumerate(single):
        to_plane(k, 1 - n % 2)
    straight(tgt.at[0, 1], 0, rows, core_send.at[0], core_recv.at[0], partner)
    for n, k in enumerate(single):
        to_plane(k, n % 2)
    for load in loads:
        load.wait()

    lane = lax.broadcasted_iota(jnp.int32, (rows, feat), 1)
    one_row = jnp.where(lax.broadcasted_iota(jnp.int32, (ONES, rows), 0) == 0, 1.0, 0.0).astype(bf16)

    def norm_of(x):
        xf = x.astype(f32)
        return jnp.sum(xf * xf, axis=1, keepdims=True)

    def prepare_target(k, c):
        x = raw(k, c)[0]
        tgt_left[k, c, :, :feat] = x * bf16(-2.0)
        tgt_left[k, c, :, feat:] = columns(norm_of(x), lane, 0, 3)
        tgt_turned[k, c, :feat] = x.astype(f32).T.astype(bf16)
        tgt_turned[k, c, feat:] = one_row

    def prepare_source(ref, slot):
        x = ref[0]
        src_right[slot, :, :feat] = x
        src_right[slot, :, feat:] = columns(norm_of(x), lane, 3, 0)

    mine = teams

    def pair(k, c, ref, slot, add, first):
        right = src_right[slot]
        target = raw(k, c)
        dist = lax.dot_general(tgt_left[k, c], right, NT, preferred_element_type=f32)
        couple = lax.dot_general(
            jnp.concatenate([target[1], target[2]], axis=1),
            jnp.concatenate([ref[2], ref[1]], axis=1),
            NT, preferred_element_type=f32,
        )
        dist = jnp.maximum(dist, 1e-30)
        power = dist * lax.rsqrt(dist) * (-RATE)
        weight = ((LOG2E - power) * jnp.exp2(power) * couple).astype(bf16)
        back = jnp.dot(tgt_turned[k, c], weight, preferred_element_type=f32)
        if first:
            turned[slot] = back
        else:
            turned[slot] += back
        if add is not None:
            forth = jnp.dot(weight, right, preferred_element_type=f32)
            if add:
                acc[k, c] += forth
            else:
                acc[k, c] = forth

    def gradient(k, c):
        total = acc[k, c]
        return GAIN * (total[:, feat:feat + 1] * raw(k, c)[0].astype(f32) - total[:, :feat])

    def turned_gradient(ref, slot):
        total = turned[slot]
        fill = jnp.zeros((feat - ONES, rows), f32)
        whole = jnp.concatenate([total, fill], axis=0).T
        return GAIN * (whole[:, feat:feat + 1] * ref[0].astype(f32) - whole[:, :feat])

    arrived = set()

    def arrive(k, h):
        if (k, h) not in arrived:
            arrived.add((k, h))
            plane_copy(k, h).wait_recv()

    def hand_on(k):
        low = k & -k
        rest = k ^ low
        arrive(rest, 0)
        plane_copy(k, 0).start()
        arrive(low if rest in single else rest, 1)
        plane_copy(k, 1).start()

    def relay(k):
        arrive(k, 0)
        arrive(k, 1)
        core_copy(k).start()

    def take(i):
        @pl.when(used(i))
        def _():
            @pl.when(jnp.logical_not(passes(i)))
            def _():
                for q in range(parts):
                    line_copy(i, q).wait_recv()
            prepare_source(src.at[i], i)

    def own_pairs(targets):
        for k, c in targets:
            prepare_target(k, c)
            pair(k, c, own, mine, None, (k, c) == (0, 0))

    def pairs(i, targets):
        @pl.when(used(i))
        def _():
            for k, c in targets:
                pair(k, c, src.at[i], i, i > 0, (k, c) == targets[0] and (k, c) in opening)

    def to_owner(i):
        return remote(
            line_out.at[i], line_in.at[team], lsum_send.at[i], lsum_recv.at[team], (blk, i),
        )

    def give_back(i):
        line_out[i] = turned_gradient(src.at[i], i).astype(bf16)
        to_owner(i).start()

    def csum_copy(k):
        return remote(core_out.at[k], core_in.at[k], csum_send.at[k], csum_recv.at[k], partner)

    def psum_copy(k):
        return remote(plane_out.at[k - 1], plane_in.at[k - 1], psum_send.at[k], psum_recv.at[k], peer[k])

    always = team >= 0
    low_half = team < teams // 2
    close = [(0, 0), (0, 1)] + [(k, 0) for k in single]
    across = [(k, 1) for k in single]
    rest = [(k, c) for c in (0, 1) for k in joint]
    opening = close[:1]
    two = [k for k in joint if bin(k).count("1") == 2]
    more = [k for k in joint if k not in two]

    prepare_source(own, mine)
    own_pairs(close[:1])
    pass_on(0, always)
    core_copy(0).wait_recv()
    own_pairs(close[1:2])
    for k in two:
        hand_on(k)
    for q in range(1, parts - 1):
        pass_on(q, always)
    pass_on(parts - 1, low_half)
    for k in single:
        relay(k)
    pass_on(parts - 1, jnp.logical_not(low_half))
    own_pairs(close[2:])

    end = team == teams - 1

    def relay_rest(condition):
        @pl.when(condition)
        def _():
            for k in two:
                for h in range(2):
                    plane_copy(k, h).wait_recv()
                core_copy(k).start()

    relay_rest(end)
    base = sources[:1]
    inner = sources[1:-1]
    final = sources[1:][-1:]
    alone, joined = team == 0, team > 0

    def own_and_base(targets):
        @pl.when(alone)
        def _():
            own_pairs(targets)

        @pl.when(joined)
        def _():
            own_pairs(targets)
            for i in base:
                for k, c in targets:
                    pair(k, c, src.at[i], i, False, False)

    for i in base:
        take(i)
        pairs(i, close)
    relay_rest(jnp.logical_not(end))
    for k in two:
        arrived.update({(k, 0), (k, 1)})
    for k in more:
        hand_on(k)
        relay(k)
    for i in inner:
        take(i)
        pairs(i, close)
    for k, c in across:
        core_copy(k).wait_recv()
    if across:
        own_and_base(across)
    for k, c in rest:
        if c:
            core_copy(k).wait_recv()

    @pl.when(alone)
    def _():
        own_pairs(rest)

    @pl.when(joined)
    def _():
        for k, c in rest:
            prepare_target(k, c)
            for i in base:
                pair(k, c, src.at[i], i, False, False)
        for i in base:
            give_back(i)

    @pl.when(joined)
    def _():
        for k, c in rest:
            pair(k, c, own, mine, None, False)
    for i in inner:
        pairs(i, across + rest)

        @pl.when(used(i))
        def _():
            give_back(i)

    for i in final:
        take(i)
    order = list(reversed(range(planes)))
    holds = used(final[0]) if final else team < 0

    def hand_over():
        for k in order:
            core_out[k] = gradient(k, 1).astype(bf16)
            csum_copy(k).start()

    def send_out():
        for k in order[:-1]:
            csum_copy(k).wait_recv()
            plane_out[k - 1] = (gradient(k, 0) + core_in[k].astype(f32)).astype(bf16)
            psum_copy(k).start()

    @pl.when(holds)
    def _():
        for i in final:
            for k in order:
                pair(k, 1, src.at[i], i, True, k == order[0])
        hand_over()
        for i in final:
            for k in order:
                pair(k, 0, src.at[i], i, True, False)
        send_out()
        for i in final:
            give_back(i)

    @pl.when(joined & jnp.logical_not(holds))
    def _():
        hand_over()
        send_out()

    out_ref[...] = turned_gradient(own, mine)

    @pl.when(joined)
    def _():
        csum_copy(0).wait_recv()
        out_ref[...] += gradient(0, 0) + core_in[0].astype(f32)
        for k in order[:-1]:
            psum_copy(k).wait_recv()
            out_ref[...] += plane_in[k - 1].astype(f32)

    for j in range(teams):
        @pl.when(uses(teams, team, j))
        def _():
            remote(line_out.at[j], line_in.at[j], lsum_send.at[j], lsum_recv.at[j], partner).wait_recv()
            out_ref[...] += line_in[j].astype(f32)

    for k in range(1, planes):
        for h in range(2):
            plane_copy(k, h).wait_send()
    for k in range(planes):
        core_copy(k).wait_send()
    for step, condition in ways:
        @pl.when(condition)
        def _():
            for q in range(parts):
                own_copy(step, q).wait_send()
    for i in sources:
        @pl.when(passes(i))
        def _():
            for q in range(parts):
                line_copy(i, q).wait_send()

        @pl.when(used(i))
        def _():
            to_owner(i).wait_send()

    @pl.when(team > 0)
    def _():
        for k in range(planes):
            csum_copy(k).wait_send()
            if k:
                psum_copy(k).wait_send()


def local(planes, teams, features, left_vectors, right_vectors):
    rows, feat = features.shape
    kind = jnp.bfloat16
    dma = pltpu.SemaphoreType.DMA
    parts = 4
    others = max(planes - 1, 1)
    return pl.pallas_call(
        functools.partial(kernel, planes, teams, parts),
        out_shape=jax.ShapeDtypeStruct((rows, feat), jnp.float32),
        in_specs=[pl.BlockSpec(memory_space=pl.ANY)] * 3,
        out_specs=pl.BlockSpec(memory_space=pltpu.VMEM),
        scratch_shapes=[
            pltpu.VMEM((3, rows, feat), kind),
            pltpu.VMEM((planes, 2, 3, rows, feat), kind),
            pltpu.VMEM((teams, 3, rows, feat), kind),
            pltpu.VMEM((planes, 2, rows, 2 * feat), kind),
            pltpu.VMEM((planes, 2, feat + ONES, rows), kind),
            pltpu.VMEM((teams + 1, rows, 2 * feat), kind),
            pltpu.VMEM((planes, 2, rows, 2 * feat), jnp.float32),
            pltpu.VMEM((teams + 1, feat + ONES, rows), jnp.float32),
            pltpu.VMEM((planes, rows, feat), kind),
            pltpu.VMEM((planes, rows, feat), kind),
            pltpu.VMEM((others, rows, feat), kind),
            pltpu.VMEM((others, rows, feat), kind),
            pltpu.VMEM((teams, rows, feat), kind),
            pltpu.VMEM((teams, rows, feat), kind),
            dma((3,)),
            dma((planes,)), dma((planes,)),
            dma((planes, 2)), dma((planes, 2)),
            dma((parts,)),
            dma((teams, parts)), dma((teams, parts)),
            dma((planes,)), dma((planes,)),
            dma((planes,)), dma((planes,)),
            dma((teams,)), dma((teams,)),
        ],
        compiler_params=pltpu.CompilerParams(
            collective_id=0, has_side_effects=True, vmem_limit_bytes=24 * 2**20,
        ),
    )(*(pltpu.with_memory_space_constraint(v, pltpu.HBM) for v in (features, left_vectors, right_vectors)))


def solution(mesh):
    spec = P(("blk", "team"), None)
    planes, teams = mesh.shape["blk"] // 2, mesh.shape["team"]
    return jax.shard_map(
        functools.partial(local, planes, teams), mesh=mesh,
        in_specs=(spec, spec, spec), out_specs=spec, check_vma=False,
    )
```

```python
import functools
import math

import jax
import jax.numpy as jnp
from jax import lax
from jax.experimental import pallas as pl
from jax.experimental.pallas import tpu as pltpu
from jax.sharding import PartitionSpec as P

MESH = pl.DeviceIdType.MESH
LOG2E = math.log2(math.e)
RATE = math.sqrt(5.0) * LOG2E
GAIN = -(5.0 / 3.0) / LOG2E
NT = (((1,), (1,)), ((), ()))
ONES = 16


def flip(index, bits):
    step = 1
    while step <= bits:
        if bits & step:
            index = index + step - 2 * step * ((index // step) % 2)
        step *= 2
    return index


def columns(norm, lane, first, ones):
    high = norm.astype(jnp.bfloat16).astype(jnp.float32)
    rest = norm - high
    mid = rest.astype(jnp.bfloat16).astype(jnp.float32)
    low = rest - mid
    out = jnp.where((lane >= ones) & (lane < ones + 3), 1.0, 0.0)
    for place, term in enumerate((high, mid, low)):
        out = jnp.where(lane == first + place, term, out)
    return out.astype(jnp.bfloat16)


def top(teams, i):
    return teams - 1 - i - jnp.minimum(i, 1)


def bottom(teams, i):
    return jnp.maximum(teams - 1 - i, 1)


def rises(teams, i):
    return i + 1 <= top(teams, i)


def sinks(teams, i):
    return i - 1 >= bottom(teams, i)


def uses(teams, i, t):
    return ((t > i) & (t <= top(teams, i))) | ((t < i) & (t >= bottom(teams, i)))


def kernel(
    planes, teams, parts, x_hbm, l_hbm, r_hbm, out_ref,
    own, tgt, src, tgt_left, tgt_turned, src_right, acc, turned,
    core_out, core_in, plane_out, plane_in, line_out, line_in,
    load_sem, core_send, core_recv, plane_send, plane_recv,
    own_send, line_send, line_recv, csum_send, csum_recv,
    psum_send, psum_recv, lsum_send, lsum_recv,
):
    blk, team = lax.axis_index("blk"), lax.axis_index("team")
    plane, core = blk // 2, blk % 2
    rows, feat = x_hbm.shape
    half, size = rows // 2, rows // parts
    bf16, f32 = jnp.bfloat16, jnp.float32

    loads = [
        pltpu.make_async_copy(ref, own.at[i], load_sem.at[i])
        for i, ref in enumerate((x_hbm, l_hbm, r_hbm))
    ]
    for load in loads:
        load.start()

    partner = (plane * 2 + 1 - core, team)
    peer = [(flip(plane, k) * 2 + core, team) for k in range(planes)]
    single = [k for k in range(1, planes) if k & (k - 1) == 0]
    joint = [k for k in range(1, planes) if k & (k - 1)]
    barrier = pltpu.get_barrier_semaphore()
    near = [partner] + [peer[k] for k in single]
    for device in near:
        pl.semaphore_signal(barrier, inc=1, device_id=device, device_id_type=MESH)
    for step in (1, -1):
        @pl.when((team + step >= 0) & (team + step < teams))
        def _():
            pl.semaphore_signal(barrier, inc=1, device_id=(blk, team + step), device_id_type=MESH)

    def remote(source, target, send, recv, device):
        return pltpu.make_async_remote_copy(
            src_ref=source, dst_ref=target, send_sem=send, recv_sem=recv,
            device_id=device, device_id_type=MESH,
        )

    def raw(k, c):
        return own if (k, c) == (0, 0) else tgt.at[k, c]

    def part(ref, h, length):
        return ref.at[:, pl.ds(h * length, length)]

    inputs = (x_hbm, l_hbm, r_hbm)

    def straight(target, h, length, send, recv, device):
        for i, ref in enumerate(inputs):
            place = pl.ds(h * length, length)
            remote(ref.at[place], target.at[i, place], send, recv, device).start()

    def plane_copy(k, h):
        if k in single:
            source, device = own, peer[k]
        else:
            low = k & -k
            rest = k ^ low
            if h and rest in single:
                source, device = raw(low, 0), peer[rest]
            else:
                source, device = raw(rest, 0), peer[low]
        return remote(
            part(source, h, half), part(tgt.at[k, 0], h, half),
            plane_send.at[k, h], plane_recv.at[k, h], device,
        )

    def core_copy(k):
        return remote(raw(k, 0), tgt.at[k, 1], core_send.at[k], core_recv.at[k], partner)

    def direction(i):
        return 1 if 2 * i < teams - 1 else -1

    def goes(i):
        near_end, far_end = min(i, teams - 1 - i), max(i, teams - 1 - i)
        if i < far_end:
            return far_end - near_end > 1 or i == 0
        return far_end - near_end > 1 or 0 < near_end < far_end

    sources = [i for i in range(teams) if teams > 1 and goes(i)]

    def used(i):
        return uses(teams, i, team)

    def passes(i):
        return used(i) & uses(teams, i, team + direction(i))

    def line_copy(i, q):
        return remote(
            part(src.at[i], q, size), part(src.at[i], q, size),
            line_send.at[i, q], line_recv.at[i, q], (blk, team + direction(i)),
        )

    def own_copy(step, q):
        return remote(
            part(own, q, size), part(src.at[team], q, size),
            own_send.at[q], line_recv.at[team, q], (blk, team + step),
        )

    ways = ((1, rises(teams, team)), (-1, sinks(teams, team)))

    def pass_on(steps, condition):
        @pl.when(condition)
        def _():
            for step in steps:
                for i in sources:
                    q = step - (direction(i) < 0)
                    if 0 <= q < parts:
                        @pl.when(passes(i))
                        def _():
                            line_copy(i, q).wait_recv()
                            line_copy(i, q).start()

    on_line = jnp.minimum(team, 1) + jnp.minimum(teams - 1 - team, 1)
    pl.semaphore_wait(barrier, len(near) + on_line)
    for step, condition in ways:
        @pl.when(condition)
        def _():
            for q in range(parts):
                straight(
                    src.at[team], q, size, own_send.at[q], line_recv.at[team, q], (blk, team + step),
                )

    def to_plane(k, h):
        straight(tgt.at[k, 0], h, half, plane_send.at[k, h], plane_recv.at[k, h], peer[k])

    for n, k in enumerate(single):
        to_plane(k, 1 - n % 2)
    straight(tgt.at[0, 1], 0, rows, core_send.at[0], core_recv.at[0], partner)
    for n, k in enumerate(single):
        to_plane(k, n % 2)
    for load in loads:
        load.wait()

    lane = lax.broadcasted_iota(jnp.int32, (rows, feat), 1)
    one_row = jnp.where(lax.broadcasted_iota(jnp.int32, (ONES, rows), 0) == 0, 1.0, 0.0).astype(bf16)

    def norm_of(x):
        xf = x.astype(f32)
        return jnp.sum(xf * xf, axis=1, keepdims=True)

    def prepare_target(k, c):
        x = raw(k, c)[0]
        tgt_left[k, c, :, :feat] = x * bf16(-2.0)
        tgt_left[k, c, :, feat:] = columns(norm_of(x), lane, 0, 3)
        tgt_turned[k, c, :feat] = x.astype(f32).T.astype(bf16)
        tgt_turned[k, c, feat:] = one_row

    def prepare_source(ref, slot):
        x = ref[0]
        src_right[slot, :, :feat] = x
        src_right[slot, :, feat:] = columns(norm_of(x), lane, 3, 0)

    mine = teams

    def products(k, c, ref, slot):
        target = raw(k, c)
        dist = lax.dot_general(
            tgt_left[k, c], src_right[slot], NT, preferred_element_type=f32,
        )
        couple = lax.dot_general(
            jnp.concatenate([target[1], target[2]], axis=1),
            jnp.concatenate([ref[2], ref[1]], axis=1),
            NT, preferred_element_type=f32,
        )
        return dist, couple

    def weight_of(dist, couple):
        dist = jnp.maximum(dist, 1e-30)
        power = dist * lax.rsqrt(dist) * (-RATE)
        return ((LOG2E - power) * jnp.exp2(power) * couple).astype(bf16)

    def gather(k, c, slot, weight, add, first):
        back = jnp.dot(tgt_turned[k, c], weight, preferred_element_type=f32)
        if first:
            turned[slot] = back
        else:
            turned[slot] += back
        if add is not None:
            forth = jnp.dot(weight, src_right[slot], preferred_element_type=f32)
            if add:
                acc[k, c] += forth
            else:
                acc[k, c] = forth

    def chain(jobs):
        ahead = None
        for n, (k, c, ref, slot, add, first) in enumerate(jobs):
            now = products(k, c, ref, slot) if ahead is None else ahead
            if n + 1 < len(jobs):
                ahead = products(*jobs[n + 1][:4])
            gather(k, c, slot, weight_of(*now), add, first)

    def with_own(targets):
        return [(k, c, own, mine, None, (k, c) == (0, 0)) for k, c in targets]

    def with_source(i, targets, add, opens=False):
        return [
            (k, c, src.at[i], i, add, opens and n == 0) for n, (k, c) in enumerate(targets)
        ]

    def gradient(k, c):
        total = acc[k, c]
        return GAIN * (total[:, feat:feat + 1] * raw(k, c)[0].astype(f32) - total[:, :feat])

    def turned_gradient(ref, slot):
        total = turned[slot]
        fill = jnp.zeros((feat - ONES, rows), f32)
        whole = jnp.concatenate([total, fill], axis=0).T
        return GAIN * (whole[:, feat:feat + 1] * ref[0].astype(f32) - whole[:, :feat])

    arrived = set()

    def arrive(k, h):
        if (k, h) not in arrived:
            arrived.add((k, h))
            plane_copy(k, h).wait_recv()

    def hand_on(k):
        low = k & -k
        rest = k ^ low
        arrive(rest, 0)
        plane_copy(k, 0).start()
        arrive(low if rest in single else rest, 1)
        plane_copy(k, 1).start()

    def relay(k):
        arrive(k, 0)
        arrive(k, 1)
        core_copy(k).start()

    def take(i):
        @pl.when(used(i))
        def _():
            @pl.when(jnp.logical_not(passes(i)))
            def _():
                for q in range(parts):
                    line_copy(i, q).wait_recv()
            prepare_source(src.at[i], i)

    def prepare(targets):
        for k, c in targets:
            prepare_target(k, c)

    def own_pairs(targets):
        prepare(targets)
        chain(with_own(targets))

    def to_owner(i):
        return remote(
            line_out.at[i], line_in.at[team], lsum_send.at[i], lsum_recv.at[team], (blk, i),
        )

    def give_back(i):
        line_out[i] = turned_gradient(src.at[i], i).astype(bf16)
        to_owner(i).start()

    def csum_copy(k):
        return remote(core_out.at[k], core_in.at[k], csum_send.at[k], csum_recv.at[k], partner)

    def psum_copy(k):
        return remote(plane_out.at[k - 1], plane_in.at[k - 1], psum_send.at[k], psum_recv.at[k], peer[k])

    always = team >= 0
    low_half = team < teams // 2
    close = [(0, 0), (0, 1)] + [(k, 0) for k in single]
    across = [(k, 1) for k in single]
    rest = [(k, c) for c in (0, 1) for k in joint]
    two = [k for k in joint if bin(k).count("1") == 2]
    more = [k for k in joint if k not in two]

    prepare_source(own, mine)
    own_pairs(close[:1])
    pass_on(range(parts // 4), always)
    core_copy(0).wait_recv()
    own_pairs(close[1:2])
    pass_on(range(parts // 4, parts // 2), low_half)
    for k in two:
        hand_on(k)
    pass_on(range(parts // 2, parts + 1), low_half)
    base = sources[:1]
    ready = (team > 0) & low_half & (team < teams - 1)

    @pl.when(ready)
    def _():
        for i in base:
            take(i)
            chain(with_source(i, close[:2], False, True))
    pass_on(range(parts // 4, 3 * parts // 4), jnp.logical_not(low_half))
    for k in single:
        relay(k)

    @pl.when(jnp.logical_not(ready))
    def _():
        own_pairs(close[2:])
    pass_on(range(3 * parts // 4, parts + 1), jnp.logical_not(low_half))

    end = team == teams - 1

    def relay_rest(condition):
        @pl.when(condition)
        def _():
            for k in two:
                for h in range(2):
                    plane_copy(k, h).wait_recv()
                core_copy(k).start()

    relay_rest(end)
    inner = sources[1:-1]
    final = sources[1:][-1:]
    alone, joined = team == 0, team > 0

    between = joined & jnp.logical_not(end)

    @pl.when(ready)
    def _():
        prepare(close[2:])
        jobs = with_own(close[2:])
        for i in base:
            jobs += with_source(i, close[2:], False)
        chain(jobs)
    for i in base:
        @pl.when(between & jnp.logical_not(ready))
        def _():
            take(i)
            chain(with_source(i, close, False, True))
    for i in inner:
        take(i)

        @pl.when(used(i))
        def _():
            chain(with_source(i, close, True, True))
    beside = (used(final[0]) & (abs(final[0] - team) == 1)) if final else team < 0
    for i in final:
        @pl.when(beside)
        def _():
            take(i)
            chain(with_source(i, close, True, True))
    relay_rest(jnp.logical_not(end))
    for k in two:
        arrived.update({(k, 0), (k, 1)})
    for k in more:
        hand_on(k)
        relay(k)
    for k, c in across:
        core_copy(k).wait_recv()

    @pl.when(jnp.logical_not(between))
    def _():
        own_pairs(across)

    @pl.when(between)
    def _():
        prepare(across)
        chain(with_own(across) + [job for i in base for job in with_source(i, across, False)])

    for k, c in rest:
        if c:
            core_copy(k).wait_recv()

    @pl.when(jnp.logical_not(between))
    def _():
        own_pairs(rest)

    @pl.when(joined & end)
    def _():
        for i in base:
            take(i)
            chain(with_source(i, close + across + rest, False, True))
            give_back(i)

    @pl.when(between)
    def _():
        prepare(rest)
        for i in base:
            chain(with_source(i, rest, False))
            give_back(i)
        chain(with_own(rest))
    for i in inner:
        @pl.when(used(i))
        def _():
            chain(with_source(i, across + rest, True))
            give_back(i)

    for i in final:
        @pl.when(jnp.logical_not(beside))
        def _():
            take(i)
    order = list(reversed(range(planes)))
    holds = used(final[0]) if final else team < 0

    def hand_over():
        for k in order:
            core_out[k] = gradient(k, 1).astype(bf16)
            csum_copy(k).start()

    def send_out():
        for k in order[:-1]:
            csum_copy(k).wait_recv()
            plane_out[k - 1] = (gradient(k, 0) + core_in[k].astype(f32)).astype(bf16)
            psum_copy(k).start()

    def finish(condition, done):
        @pl.when(condition)
        def _():
            for i in final:
                targets = [(k, 1) for k in order if (k, 1) not in done]
                chain(with_source(i, targets, True, not done))
            hand_over()
            for i in final:
                targets = [(k, 0) for k in order if (k, 0) not in done]
                chain(with_source(i, targets, True))
            send_out()
            for i in final:
                give_back(i)

    finish(holds & beside, close)
    finish(holds & jnp.logical_not(beside), [])

    @pl.when(joined & jnp.logical_not(holds))
    def _():
        hand_over()
        send_out()

    out_ref[...] = turned_gradient(own, mine)

    @pl.when(joined)
    def _():
        csum_copy(0).wait_recv()
        out_ref[...] += gradient(0, 0) + core_in[0].astype(f32)
        for k in order[:-1]:
            psum_copy(k).wait_recv()
            out_ref[...] += plane_in[k - 1].astype(f32)

    for j in range(teams):
        @pl.when(uses(teams, team, j))
        def _():
            remote(line_out.at[j], line_in.at[j], lsum_send.at[j], lsum_recv.at[j], partner).wait_recv()
            out_ref[...] += line_in[j].astype(f32)

    for k in range(1, planes):
        for h in range(2):
            plane_copy(k, h).wait_send()
    for k in range(planes):
        core_copy(k).wait_send()
    for step, condition in ways:
        @pl.when(condition)
        def _():
            for q in range(parts):
                own_copy(step, q).wait_send()
    for i in sources:
        @pl.when(passes(i))
        def _():
            for q in range(parts):
                line_copy(i, q).wait_send()

        @pl.when(used(i))
        def _():
            to_owner(i).wait_send()

    @pl.when(team > 0)
    def _():
        for k in range(planes):
            csum_copy(k).wait_send()
            if k:
                psum_copy(k).wait_send()


def local(planes, teams, features, left_vectors, right_vectors):
    rows, feat = features.shape
    kind = jnp.bfloat16
    dma = pltpu.SemaphoreType.DMA
    parts = math.gcd(rows // 16, 4)
    others = max(planes - 1, 1)
    return pl.pallas_call(
        functools.partial(kernel, planes, teams, parts),
        out_shape=jax.ShapeDtypeStruct((rows, feat), jnp.float32),
        in_specs=[pl.BlockSpec(memory_space=pl.ANY)] * 3,
        out_specs=pl.BlockSpec(memory_space=pltpu.VMEM),
        scratch_shapes=[
            pltpu.VMEM((3, rows, feat), kind),
            pltpu.VMEM((planes, 2, 3, rows, feat), kind),
            pltpu.VMEM((teams, 3, rows, feat), kind),
            pltpu.VMEM((planes, 2, rows, 2 * feat), kind),
            pltpu.VMEM((planes, 2, feat + ONES, rows), kind),
            pltpu.VMEM((teams + 1, rows, 2 * feat), kind),
            pltpu.VMEM((planes, 2, rows, 2 * feat), jnp.float32),
            pltpu.VMEM((teams + 1, feat + ONES, rows), jnp.float32),
            pltpu.VMEM((planes, rows, feat), kind),
            pltpu.VMEM((planes, rows, feat), kind),
            pltpu.VMEM((others, rows, feat), kind),
            pltpu.VMEM((others, rows, feat), kind),
            pltpu.VMEM((teams, rows, feat), kind),
            pltpu.VMEM((teams, rows, feat), kind),
            dma((3,)),
            dma((planes,)), dma((planes,)),
            dma((planes, 2)), dma((planes, 2)),
            dma((parts,)),
            dma((teams, parts)), dma((teams, parts)),
            dma((planes,)), dma((planes,)),
            dma((planes,)), dma((planes,)),
            dma((teams,)), dma((teams,)),
        ],
        compiler_params=pltpu.CompilerParams(
            collective_id=0, has_side_effects=True, vmem_limit_bytes=24 * 2**20,
        ),
    )(*(pltpu.with_memory_space_constraint(v, pltpu.HBM) for v in (features, left_vectors, right_vectors)))


def solution(mesh):
    spec = P(("blk", "team"), None)
    planes, teams = mesh.shape["blk"] // 2, mesh.shape["team"]
    return jax.shard_map(
        functools.partial(local, planes, teams), mesh=mesh,
        in_specs=(spec, spec, spec), out_specs=spec, check_vma=False,
    )
```

```python
import functools
import math

import jax
import jax.numpy as jnp
from jax import lax
from jax.experimental import pallas as pl
from jax.experimental.pallas import tpu as pltpu
from jax.sharding import PartitionSpec as P

MESH = pl.DeviceIdType.MESH
LOG2E = math.log2(math.e)
RATE = math.sqrt(5.0) * LOG2E
GAIN = -(5.0 / 3.0) / LOG2E
NT = (((1,), (1,)), ((), ()))
ONES = 16


def flip(index, bits):
    step = 1
    while step <= bits:
        if bits & step:
            index = index + step - 2 * step * ((index // step) % 2)
        step *= 2
    return index


def columns(norm, lane, first, ones):
    high = norm.astype(jnp.bfloat16).astype(jnp.float32)
    rest = norm - high
    mid = rest.astype(jnp.bfloat16).astype(jnp.float32)
    low = rest - mid
    out = jnp.where((lane >= ones) & (lane < ones + 3), 1.0, 0.0)
    for place, term in enumerate((high, mid, low)):
        out = jnp.where(lane == first + place, term, out)
    return out.astype(jnp.bfloat16)


def top(teams, i):
    return teams - 1 - i - jnp.minimum(i, 1)


def bottom(teams, i):
    return jnp.maximum(teams - 1 - i, 1)


def rises(teams, i):
    return i + 1 <= top(teams, i)


def sinks(teams, i):
    return i - 1 >= bottom(teams, i)


def uses(teams, i, t):
    return ((t > i) & (t <= top(teams, i))) | ((t < i) & (t >= bottom(teams, i)))


def kernel(
    planes, teams, parts, x_hbm, l_hbm, r_hbm, out_ref,
    own, tgt, src, tgt_left, tgt_turned, src_right, acc, turned,
    core_out, core_in, plane_out, plane_in, line_out, line_in,
    load_sem, core_send, core_recv, plane_send, plane_recv,
    own_send, line_send, line_recv, csum_send, csum_recv,
    psum_send, psum_recv, lsum_send, lsum_recv,
):
    blk, team = lax.axis_index("blk"), lax.axis_index("team")
    plane, core = blk // 2, blk % 2
    rows, feat = x_hbm.shape
    half, size = rows // 2, rows // parts
    bf16, f32 = jnp.bfloat16, jnp.float32

    loads = [
        pltpu.make_async_copy(ref, own.at[i], load_sem.at[i])
        for i, ref in enumerate((x_hbm, l_hbm, r_hbm))
    ]
    for load in loads:
        load.start()

    partner = (plane * 2 + 1 - core, team)
    peer = [(flip(plane, k) * 2 + core, team) for k in range(planes)]
    single = [k for k in range(1, planes) if k & (k - 1) == 0]
    joint = [k for k in range(1, planes) if k & (k - 1)]
    barrier = pltpu.get_barrier_semaphore()
    near = [partner] + [peer[k] for k in single]
    for device in near:
        pl.semaphore_signal(barrier, inc=1, device_id=device, device_id_type=MESH)
    for step in (1, -1):
        @pl.when((team + step >= 0) & (team + step < teams))
        def _():
            pl.semaphore_signal(barrier, inc=1, device_id=(blk, team + step), device_id_type=MESH)

    def remote(source, target, send, recv, device):
        return pltpu.make_async_remote_copy(
            src_ref=source, dst_ref=target, send_sem=send, recv_sem=recv,
            device_id=device, device_id_type=MESH,
        )

    def raw(k, c):
        return own if (k, c) == (0, 0) else tgt.at[k, c]

    def part(ref, h, length):
        return ref.at[:, pl.ds(h * length, length)]

    inputs = (x_hbm, l_hbm, r_hbm)

    def straight(target, h, length, send, recv, device):
        for i, ref in enumerate(inputs):
            place = pl.ds(h * length, length)
            remote(ref.at[place], target.at[i, place], send, recv, device).start()

    def plane_copy(k, h):
        if k in single:
            source, device = own, peer[k]
        else:
            low = k & -k
            rest = k ^ low
            if h and rest in single:
                source, device = raw(low, 0), peer[rest]
            else:
                source, device = raw(rest, 0), peer[low]
        return remote(
            part(source, h, half), part(tgt.at[k, 0], h, half),
            plane_send.at[k, h], plane_recv.at[k, h], device,
        )

    def core_copy(k):
        return remote(raw(k, 0), tgt.at[k, 1], core_send.at[k], core_recv.at[k], partner)

    def direction(i):
        return 1 if 2 * i < teams - 1 else -1

    def goes(i):
        near_end, far_end = min(i, teams - 1 - i), max(i, teams - 1 - i)
        if i < far_end:
            return far_end - near_end > 1 or i == 0
        return far_end - near_end > 1 or 0 < near_end < far_end

    sources = [i for i in range(teams) if teams > 1 and goes(i)]

    def used(i):
        return uses(teams, i, team)

    def passes(i):
        return used(i) & uses(teams, i, team + direction(i))

    def line_copy(i, q):
        return remote(
            part(src.at[i], q, size), part(src.at[i], q, size),
            line_send.at[i, q], line_recv.at[i, q], (blk, team + direction(i)),
        )

    def own_copy(step, q):
        return remote(
            part(own, q, size), part(src.at[team], q, size),
            own_send.at[q], line_recv.at[team, q], (blk, team + step),
        )

    ways = ((1, rises(teams, team)), (-1, sinks(teams, team)))

    def pass_on(steps, condition):
        @pl.when(condition)
        def _():
            for step in steps:
                for i in sources:
                    q = step - (direction(i) < 0)
                    if 0 <= q < parts:
                        @pl.when(passes(i))
                        def _():
                            line_copy(i, q).wait_recv()
                            line_copy(i, q).start()

    on_line = jnp.minimum(team, 1) + jnp.minimum(teams - 1 - team, 1)
    pl.semaphore_wait(barrier, len(near) + on_line)
    for step, condition in ways:
        @pl.when(condition)
        def _():
            for q in range(parts):
                straight(
                    src.at[team], q, size, own_send.at[q], line_recv.at[team, q], (blk, team + step),
                )

    def to_plane(k, h):
        straight(tgt.at[k, 0], h, half, plane_send.at[k, h], plane_recv.at[k, h], peer[k])

    for n, k in enumerate(single):
        to_plane(k, 1 - n % 2)
    straight(tgt.at[0, 1], 0, rows, core_send.at[0], core_recv.at[0], partner)
    for n, k in enumerate(single):
        to_plane(k, n % 2)
    for load in loads:
        load.wait()

    lane = lax.broadcasted_iota(jnp.int32, (rows, feat), 1)
    one_row = jnp.where(lax.broadcasted_iota(jnp.int32, (ONES, rows), 0) == 0, 1.0, 0.0).astype(bf16)

    def norm_of(x):
        xf = x.astype(f32)
        return jnp.sum(xf * xf, axis=1, keepdims=True)

    def prepare_target(k, c):
        x = raw(k, c)[0]
        tgt_left[k, c, :, :feat] = x * bf16(-2.0)
        tgt_left[k, c, :, feat:] = columns(norm_of(x), lane, 0, 3)
        tgt_turned[k, c, :feat] = x.astype(f32).T.astype(bf16)
        tgt_turned[k, c, feat:] = one_row

    def prepare_source(ref, slot):
        x = ref[0]
        src_right[slot, :, :feat] = x
        src_right[slot, :, feat:] = columns(norm_of(x), lane, 3, 0)

    mine = teams

    def products(k, c, ref, slot):
        target = raw(k, c)
        dist = lax.dot_general(
            tgt_left[k, c], src_right[slot], NT, preferred_element_type=f32,
        )
        couple = lax.dot_general(
            jnp.concatenate([target[1], target[2]], axis=1),
            jnp.concatenate([ref[2], ref[1]], axis=1),
            NT, preferred_element_type=f32,
        )
        return dist, couple

    def weight_of(dist, couple):
        dist = jnp.maximum(dist, 1e-30)
        power = dist * lax.rsqrt(dist) * (-RATE)
        return ((LOG2E - power) * jnp.exp2(power) * couple).astype(bf16)

    def gather(k, c, slot, weight, add, first):
        back = jnp.dot(tgt_turned[k, c], weight, preferred_element_type=f32)
        if first:
            turned[slot] = back
        else:
            turned[slot] += back
        if add is not None:
            forth = jnp.dot(weight, src_right[slot], preferred_element_type=f32)
            if add:
                acc[k, c] += forth
            else:
                acc[k, c] = forth

    def chain(jobs, after=None, then=None):
        ahead = None
        for n, (k, c, ref, slot, add, first) in enumerate(jobs):
            now = products(k, c, ref, slot) if ahead is None else ahead
            if n + 1 < len(jobs):
                ahead = products(*jobs[n + 1][:4])
            gather(k, c, slot, weight_of(*now), add, first)
            if n + 1 == after:
                then()

    def with_own(targets):
        return [(k, c, own, mine, None, (k, c) == (0, 0)) for k, c in targets]

    def with_source(i, targets, add, opens=False):
        return [
            (k, c, src.at[i], i, add, opens and n == 0) for n, (k, c) in enumerate(targets)
        ]

    def gradient(k, c):
        total = acc[k, c]
        return GAIN * (total[:, feat:feat + 1] * raw(k, c)[0].astype(f32) - total[:, :feat])

    def turned_gradient(ref, slot):
        total = turned[slot]
        fill = jnp.zeros((feat - ONES, rows), f32)
        whole = jnp.concatenate([total, fill], axis=0).T
        return GAIN * (whole[:, feat:feat + 1] * ref[0].astype(f32) - whole[:, :feat])

    arrived = set()

    def arrive(k, h):
        if (k, h) not in arrived:
            arrived.add((k, h))
            plane_copy(k, h).wait_recv()

    def hand_on(k):
        low = k & -k
        rest = k ^ low
        arrive(rest, 0)
        plane_copy(k, 0).start()
        arrive(low if rest in single else rest, 1)
        plane_copy(k, 1).start()

    def relay(k):
        arrive(k, 0)
        arrive(k, 1)
        core_copy(k).start()

    def take(i):
        @pl.when(used(i))
        def _():
            @pl.when(jnp.logical_not(passes(i)))
            def _():
                for q in range(parts):
                    line_copy(i, q).wait_recv()
            prepare_source(src.at[i], i)

    def prepare(targets):
        for k, c in targets:
            prepare_target(k, c)

    def own_pairs(targets):
        prepare(targets)
        chain(with_own(targets))

    def to_owner(i):
        return remote(
            line_out.at[i], line_in.at[team], lsum_send.at[i], lsum_recv.at[team], (blk, i),
        )

    def give_back(i):
        line_out[i] = turned_gradient(src.at[i], i).astype(bf16)
        to_owner(i).start()

    def csum_copy(k):
        return remote(core_out.at[k], core_in.at[k], csum_send.at[k], csum_recv.at[k], partner)

    def psum_copy(k):
        return remote(plane_out.at[k - 1], plane_in.at[k - 1], psum_send.at[k], psum_recv.at[k], peer[k])

    always = team >= 0
    low_half = team < teams // 2
    close = [(0, 0), (0, 1)] + [(k, 0) for k in single]
    across = [(k, 1) for k in single]
    rest = [(k, c) for c in (0, 1) for k in joint]
    two = [k for k in joint if bin(k).count("1") == 2]
    more = [k for k in joint if k not in two]

    prepare_source(own, mine)
    own_pairs(close[:1])
    pass_on(range(parts // 4), always)
    core_copy(0).wait_recv()
    own_pairs(close[1:2])
    pass_on(range(parts // 4, parts // 2), low_half)
    for k in two:
        hand_on(k)
    pass_on(range(parts // 2, parts + 1), low_half)
    base = sources[:1]
    ready = (team > 0) & low_half & (team < teams - 1)

    @pl.when(ready)
    def _():
        for i in base:
            take(i)
            chain(with_source(i, close[:2], False, True))
    pass_on(range(parts // 4, 3 * parts // 4), jnp.logical_not(low_half))
    for k in single:
        relay(k)

    @pl.when(jnp.logical_not(ready))
    def _():
        own_pairs(close[2:])
    pass_on(range(3 * parts // 4, parts + 1), jnp.logical_not(low_half))

    end = team == teams - 1

    def relay_rest(condition):
        @pl.when(condition)
        def _():
            for k in two:
                for h in range(2):
                    plane_copy(k, h).wait_recv()
                core_copy(k).start()

    relay_rest(end)
    inner = sources[1:-1]
    final = sources[1:][-1:]
    alone, joined = team == 0, team > 0

    between = joined & jnp.logical_not(end)

    @pl.when(ready)
    def _():
        prepare(close[2:])
        for i in base:
            chain(with_source(i, close[2:], False))
    for i in base:
        @pl.when(between & jnp.logical_not(ready))
        def _():
            take(i)
            chain(with_source(i, close, False, True))
    for i in inner:
        take(i)

        @pl.when(used(i))
        def _():
            chain(with_source(i, close, True, True))
    beside = (used(final[0]) & (abs(final[0] - team) == 1)) if final else team < 0
    for i in final:
        @pl.when(beside)
        def _():
            take(i)
            chain(with_source(i, close, True, True))
    relay_rest(jnp.logical_not(end))
    for k in two:
        arrived.update({(k, 0), (k, 1)})
    for k in more:
        hand_on(k)
        relay(k)
    never = team < 0
    lone, others = (inner, []) if len(inner) == 1 else ([], inner)
    rich = (between & used(lone[0])) if lone else never
    side = between & beside & jnp.logical_not(rich)
    plain = between & jnp.logical_not(rich) & jnp.logical_not(side)
    modes = ((rich, lone), (side, final), (plain, []))
    for k, c in across:
        core_copy(k).wait_recv()

    @pl.when(alone)
    def _():
        own_pairs(across)

    for mode, more_sources in modes:
        @pl.when(mode)
        def _():
            prepare(across)
            jobs = []
            for i in base:
                jobs += with_source(i, across, False)
            for i in more_sources:
                jobs += with_source(i, across, True)
            chain(jobs)

    for k, c in rest:
        if c:
            core_copy(k).wait_recv()

    @pl.when(alone)
    def _():
        own_pairs(rest)

    def base_back():
        for i in base:
            give_back(i)

    @pl.when(joined & end)
    def _():
        prepare(across + rest)
        for i in base:
            take(i)
            chain(with_source(i, close + across + rest, False, True))
        base_back()

    @pl.when(plain | side)
    def _():
        prepare(rest)
        for i in base:
            chain(with_source(i, rest, False))
        base_back()

    @pl.when(rich)
    def _():
        prepare(rest)
        jobs = []
        for i in base:
            jobs += with_source(i, rest, False)
        for i in lone:
            jobs += with_source(i, rest, True)
        chain(jobs, len(rest), base_back)
        for i in lone:
            give_back(i)
    for i in others:
        @pl.when(used(i))
        def _():
            chain(with_source(i, across + rest, True))
            give_back(i)

    for i in final:
        @pl.when(jnp.logical_not(beside))
        def _():
            take(i)
    order = list(reversed(range(planes)))
    holds = used(final[0]) if final else team < 0

    def hand_over():
        for k in order:
            core_out[k] = gradient(k, 1).astype(bf16)
            csum_copy(k).start()

    def send_out():
        for k in order[:-1]:
            csum_copy(k).wait_recv()
            plane_out[k - 1] = (gradient(k, 0) + core_in[k].astype(f32)).astype(bf16)
            psum_copy(k).start()

    def finish(condition, done, own_between):
        @pl.when(condition)
        def _():
            for i in final:
                targets = [(k, 1) for k in order if (k, 1) not in done]
                chain(with_source(i, targets, True, not done))
            hand_over()
            jobs = []
            for i in final:
                targets = [(k, 0) for k in order if (k, 0) not in done]
                jobs += with_source(i, targets, True)
            chain(jobs + with_own(own_between))
            send_out()
            for i in final:
                give_back(i)

    finish(side, close + across, across)
    finish(holds & beside & jnp.logical_not(side), close, [])
    finish(holds & jnp.logical_not(beside), [], [])

    @pl.when(joined & jnp.logical_not(holds))
    def _():
        hand_over()

        @pl.when(end)
        def _():
            chain(with_own(across + rest))
        send_out()

    for mode, targets in (
        (ready & jnp.logical_not(side), close[2:] + across + rest),
        (ready & side, close[2:] + rest),
        (between & jnp.logical_not(ready) & side, rest),
        (between & jnp.logical_not(ready) & jnp.logical_not(side), across + rest),
    ):
        @pl.when(mode)
        def _():
            chain(with_own(targets))

    out_ref[...] = turned_gradient(own, mine)

    @pl.when(joined)
    def _():
        csum_copy(0).wait_recv()
        out_ref[...] += gradient(0, 0) + core_in[0].astype(f32)
        for k in order[:-1]:
            psum_copy(k).wait_recv()
            out_ref[...] += plane_in[k - 1].astype(f32)

    for j in range(teams):
        @pl.when(uses(teams, team, j))
        def _():
            remote(line_out.at[j], line_in.at[j], lsum_send.at[j], lsum_recv.at[j], partner).wait_recv()
            out_ref[...] += line_in[j].astype(f32)

    for k in range(1, planes):
        for h in range(2):
            plane_copy(k, h).wait_send()
    for k in range(planes):
        core_copy(k).wait_send()
    for step, condition in ways:
        @pl.when(condition)
        def _():
            for q in range(parts):
                own_copy(step, q).wait_send()
    for i in sources:
        @pl.when(passes(i))
        def _():
            for q in range(parts):
                line_copy(i, q).wait_send()

        @pl.when(used(i))
        def _():
            to_owner(i).wait_send()

    @pl.when(team > 0)
    def _():
        for k in range(planes):
            csum_copy(k).wait_send()
            if k:
                psum_copy(k).wait_send()


def local(planes, teams, features, left_vectors, right_vectors):
    rows, feat = features.shape
    kind = jnp.bfloat16
    dma = pltpu.SemaphoreType.DMA
    parts = math.gcd(rows // 16, 4)
    others = max(planes - 1, 1)
    return pl.pallas_call(
        functools.partial(kernel, planes, teams, parts),
        out_shape=jax.ShapeDtypeStruct((rows, feat), jnp.float32),
        in_specs=[pl.BlockSpec(memory_space=pl.ANY)] * 3,
        out_specs=pl.BlockSpec(memory_space=pltpu.VMEM),
        scratch_shapes=[
            pltpu.VMEM((3, rows, feat), kind),
            pltpu.VMEM((planes, 2, 3, rows, feat), kind),
            pltpu.VMEM((teams, 3, rows, feat), kind),
            pltpu.VMEM((planes, 2, rows, 2 * feat), kind),
            pltpu.VMEM((planes, 2, feat + ONES, rows), kind),
            pltpu.VMEM((teams + 1, rows, 2 * feat), kind),
            pltpu.VMEM((planes, 2, rows, 2 * feat), jnp.float32),
            pltpu.VMEM((teams + 1, feat + ONES, rows), jnp.float32),
            pltpu.VMEM((planes, rows, feat), kind),
            pltpu.VMEM((planes, rows, feat), kind),
            pltpu.VMEM((others, rows, feat), kind),
            pltpu.VMEM((others, rows, feat), kind),
            pltpu.VMEM((teams, rows, feat), kind),
            pltpu.VMEM((teams, rows, feat), kind),
            dma((3,)),
            dma((planes,)), dma((planes,)),
            dma((planes, 2)), dma((planes, 2)),
            dma((parts,)),
            dma((teams, parts)), dma((teams, parts)),
            dma((planes,)), dma((planes,)),
            dma((planes,)), dma((planes,)),
            dma((teams,)), dma((teams,)),
        ],
        compiler_params=pltpu.CompilerParams(
            collective_id=0, has_side_effects=True, vmem_limit_bytes=24 * 2**20,
        ),
    )(*(pltpu.with_memory_space_constraint(v, pltpu.HBM) for v in (features, left_vectors, right_vectors)))


def solution(mesh):
    spec = P(("blk", "team"), None)
    planes, teams = mesh.shape["blk"] // 2, mesh.shape["team"]
    return jax.shard_map(
        functools.partial(local, planes, teams), mesh=mesh,
        in_specs=(spec, spec, spec), out_specs=spec, check_vma=False,
    )
```
